32 devices in a mesh: member: 2 (over x), row: 16 (over z, y, core).
Axes of the slice: x: 2, y: 2, z: 4, core: 2. Of those that a mesh axis runs over, the one named last changes fastest.
Arguments:
- innovation: bfloat16 [8, 1024, 2048], P('member', 'row'), parts along dimension 0, may hold values from -6 to 6
- background: bfloat16 [8, 1024, 2048], P('member', 'row'), parts along dimension 0, may hold values from -6 to 6
- level_weight: float32 [4], replicated, may hold values from 0.25 to 4
Outputs:
- displacement: float32 [4, 1024, 2048], P('member', 'row'), parts along dimension 0
The draws below stay inside these ranges and needn't reach their ends.
There are 2 independent parts, one for each index of `member`. The reference program is written for one: setup_inputs(seed, part) draws one part's arguments, and reference() takes and returns one part's arrays. A program takes and returns all parts, laid end to end along the dimension named above; an argument that names none is the same for every part. Nothing has to cross between parts.
All inputs are finite; a program needn't handle non-finite values.
Results may differ from the reference program's by a relative error of at most 0.0003.
Values may be sent and summed in bfloat16 or wider, within the bound.
A program may use at most 64 MiB of HBM per device.

```python
import math
import jax
import jax.numpy as jnp
from jax import lax

LEV = 4
NX = 2048
HALF = 64
SIGMA = 64
NY = 1024


def steps_of(rng, shape, split, least, top_value):
    def one(dim, shards_of):
        steps = jax.random.uniform(jax.random.fold_in(jax.random.fold_in(rng, 6), dim), (shards_of,), jnp.float32, least / len(split), top_value / len(split))
        return jnp.repeat(jnp.exp(steps), shape[dim] // shards_of).reshape((-1,) + (1,) * (len(shape) - dim - 1))

    gain = one(*split[0])
    for cut in split[1:]:
        gain = gain * one(*cut)
    return gain


def noise(own_key, dims, scale, most, pieces=(), kind=jnp.bfloat16):
    level = steps_of(own_key, dims, pieces, -0.22, 0.18) if pieces else 1.0
    values = jax.random.normal(own_key, dims, jnp.float32) * scale * level
    return jnp.minimum(jnp.maximum(values, -most), most).astype(kind)


def setup_inputs(seed: int = 0, part: int = 0) -> dict:
    key_of = jax.random.split(jax.random.key(seed), 4)
    part_splits = jax.random.split(jax.random.fold_in(key_of[3], part), 4)
    innovation = noise(part_splits[0], (LEV, NY, NX), 1.0, 6.0, ((1, 16),))
    background = noise(part_splits[1], (LEV, NY, NX), 1.0, 6.0, ((1, 16),))
    level_weight = jnp.clip(jnp.exp(jax.random.uniform(key_of[2], (LEV,), jnp.float32, math.log(0.25), math.log(4.0))), 0.25, 4.0)
    return dict(innovation=innovation, background=background, level_weight=level_weight)


def tap_at(offset):
    grid = jnp.arange(-HALF, HALF + 1).astype(jnp.float32)
    spread = jnp.float32(SIGMA)
    total = jnp.sqrt(jnp.sum(jnp.exp(-grid * grid / (spread * spread))))
    off = offset.astype(jnp.float32)
    value = jnp.exp(-off * off / (2.0 * spread * spread)) / total
    return jnp.where(jnp.abs(offset) <= HALF, value, jnp.float32(0.0))

def band_blocks():
    inner = jnp.arange(128)[:, None]
    outer = jnp.arange(128)[None, :]
    return [tap_at(128 * shift + inner - outer) for shift in (-1, 0, 1)]

def smooth_last(values, blocks):
    lead = values.shape[:-1]
    length = values.shape[-1]
    nblocks = length // 128
    widths = [(0, 0)] * (values.ndim - 1) + [(128, 128)]
    padded = jnp.pad(values, widths).reshape(lead + (nblocks + 2, 128))
    total = jnp.zeros(lead + (nblocks, 128), jnp.float32)
    for index in range(3):
        part = padded[..., index:index + nblocks, :]
        total = total + jnp.dot(part, blocks[index], precision=lax.Precision.HIGHEST, preferred_element_type=jnp.float32)
    return total.reshape(lead + (length,))

def smooth_mid(values, blocks):
    chans, length, width = values.shape
    nblocks = length // 128
    padded = jnp.pad(values, ((0, 0), (128, 128), (0, 0))).reshape(chans, nblocks + 2, 128, width)
    total = jnp.zeros((chans, nblocks, 128, width), jnp.float32)
    for index in range(3):
        part = padded[:, index:index + nblocks]
        total = total + jnp.einsum('cbix,io->cbox', part, blocks[index], precision=lax.Precision.HIGHEST, preferred_element_type=jnp.float32)
    return total.reshape(chans, length, width)

def reference(innovation, background, level_weight):
    ny = innovation.shape[1]
    nx = innovation.shape[2]

    def level_step(carry, inputs):
        numer_y, numer_x, denom = carry
        inno, back, lw = inputs
        inno = inno.astype(jnp.float32)
        back = back.astype(jnp.float32)
        padded = jnp.pad(back, 1)
        grad_y = 0.5 * (padded[2:, 1:-1] - padded[:-2, 1:-1])
        grad_x = 0.5 * (padded[1:-1, 2:] - padded[1:-1, :-2])
        numer_y = numer_y + lw * inno * grad_y
        numer_x = numer_x + lw * inno * grad_x
        denom = denom + lw * (grad_y * grad_y + grad_x * grad_x)
        return ((numer_y, numer_x, denom), None)
    zeros = jnp.zeros((ny, nx), jnp.float32)
    start = (zeros, zeros, zeros + jnp.float32(1.0))
    (numer_y, numer_x, denom), _ = lax.scan(level_step, start, (innovation, background, level_weight))
    raw = jnp.stack([numer_y / denom, numer_x / denom])
    blocks = band_blocks()
    zonal = smooth_last(raw, blocks)
    return smooth_mid(zonal, blocks)
```

```python
import jax
import jax.numpy as jnp
from jax import lax
from jax.experimental import pallas as pl
from jax.experimental.pallas import tpu as pltpu
from jax.sharding import PartitionSpec as P

HALF = 64
SIGMA = 64
LANES = 128
CHUNK = 512
GROUP = 16
WIDE = 256
SCALE = 4096.0


def tap_at(offset):
    grid = lax.broadcasted_iota(jnp.int32, (8, 2 * LANES), 1) - HALF
    off = grid.astype(jnp.float32)
    spread = jnp.float32(SIGMA)
    squares = jnp.where(grid <= HALF, jnp.exp(-off * off / (spread * spread)), 0.0)
    total = jnp.sqrt(jnp.sum(squares[:1], axis=1, keepdims=True))
    value = offset.astype(jnp.float32)
    value = jnp.exp(-value * value / (2.0 * spread * spread)) / total
    return jnp.where(jnp.abs(offset) <= HALF, value, 0.0)


def halves(value):
    high = value.astype(jnp.bfloat16)
    return high, (value - high.astype(jnp.float32)).astype(jnp.bfloat16)


def encode(raw):
    value = raw * SCALE
    value2 = value * value
    value4 = value2 * value2
    value8 = value4 * value4
    return jnp.where(value < 0.0, -value8, value8).astype(jnp.bfloat16)


def decode(code):
    code = code.astype(jnp.float32)
    size = jnp.exp2(jnp.log2(jnp.abs(code)) * 0.125) * (1.0 / SCALE)
    return jnp.where(code < 0.0, -size, size)


def kernel(
    count, inn_hbm, bg_hbm, lw_ref, out_ref,
    inn, bg, rim, edge_out, edge_in, code_out, code_in, dhigh, dlow,
    mhigh, mlow, whigh, wboth, bhigh, blow,
    in_sem, edge_send, edge_recv, send_sem, recv_sem,
):
    levels, rows, cols = inn.shape
    chunks = cols // CHUNK
    me = lax.axis_index("row")
    has = (me > 0, me < count - 1)
    peer = (jnp.maximum(me - 1, 0), jnp.minimum(me + 1, count - 1))

    load_bg = pltpu.make_async_copy(bg_hbm, bg, in_sem.at[0])
    load_inn = pltpu.make_async_copy(inn_hbm, inn, in_sem.at[1])
    load_bg.start()
    load_inn.start()
    barrier = pltpu.get_barrier_semaphore()
    for side in (0, 1):
        @pl.when(has[side])
        def _():
            pl.semaphore_signal(
                barrier, inc=1, device_id={"row": peer[side]},
                device_id_type=pl.DeviceIdType.MESH,
            )

    zeros = jnp.zeros((levels, rows + 16, LANES), jnp.float32)
    rim[:, :, :LANES] = zeros
    rim[:, :, LANES + cols :] = zeros
    strip = jnp.zeros((2 * rows, LANES), jnp.bfloat16)
    for ref in (mhigh, mlow):
        ref[:, :LANES] = strip
        ref[:, LANES + cols :] = strip

    load_bg.wait()
    for level in range(levels):
        edge_out[0, level : level + 1, :] = bg[level, :16, :].astype(jnp.float32)[:1]
        edge_out[1, level : level + 1, :] = bg[level, rows - 16 :, :].astype(jnp.float32)[15:]
    pl.semaphore_wait(barrier, peer[1] - peer[0])

    def edge_copy(side):
        return pltpu.make_async_remote_copy(
            src_ref=edge_out.at[side], dst_ref=edge_in.at[1 - side],
            send_sem=edge_send.at[side], recv_sem=edge_recv.at[1 - side],
            device_id={"row": peer[side]}, device_id_type=pl.DeviceIdType.MESH,
        )

    def code_copy(side, chunk):
        return pltpu.make_async_remote_copy(
            src_ref=code_out.at[chunk], dst_ref=code_in.at[1 - side, chunk],
            send_sem=send_sem.at[side, chunk], recv_sem=recv_sem.at[1 - side, chunk],
            device_id={"row": peer[side]}, device_id_type=pl.DeviceIdType.MESH,
        )

    for side in (0, 1):
        @pl.when(has[side])
        def _():
            edge_copy(side).start()

    @pl.loop(0, chunks)
    def _(chunk):
        at = pl.multiple_of(chunk * CHUNK, CHUNK)
        for level in range(levels):
            rim[level, 8 : 8 + rows, pl.ds(LANES + at, CHUNK)] = bg[
                level, :, pl.ds(at, CHUNK)
            ].astype(jnp.float32)

    load_inn.wait()

    def raw_tile(group, chunk):
        at = pl.multiple_of(chunk * CHUNK, CHUNK)
        top = 8 + group * GROUP
        wide = CHUNK + 2 * LANES
        numer_y = numer_x = None
        denom = jnp.ones((GROUP, CHUNK), jnp.float32)
        for level in range(levels):
            weight = lw_ref[level]
            line = rim[level, top : top + GROUP, pl.ds(at, wide)]
            left = pltpu.roll(line, 1, 1)[:, LANES : LANES + CHUNK]
            right = pltpu.roll(line, wide - 1, 1)[:, LANES : LANES + CHUNK]
            above = rim[level, top - 1 : top - 1 + GROUP, pl.ds(LANES + at, CHUNK)]
            below = rim[level, top + 1 : top + 1 + GROUP, pl.ds(LANES + at, CHUNK)]
            grad_x = 0.5 * (right - left)
            grad_y = 0.5 * (below - above)
            span = pl.ds(group * GROUP, GROUP)
            scaled = weight * inn[level, span, pl.ds(at, CHUNK)].astype(jnp.float32)
            part_y, part_x = scaled * grad_y, scaled * grad_x
            numer_y = part_y if numer_y is None else numer_y + part_y
            numer_x = part_x if numer_x is None else numer_x + part_x
            denom = denom + weight * (grad_y * grad_y + grad_x * grad_x)
        inverse = 1.0 / denom
        for comp, numer in enumerate((numer_y, numer_x)):
            raw = numer * inverse
            low_row = comp * rows + group * GROUP
            code_out[chunk, low_row : low_row + GROUP, :] = encode(raw)
            high, low = halves(raw)
            base = rows + group * GROUP
            dhigh[comp, base : base + GROUP, pl.ds(at, CHUNK)] = high
            dlow[comp, base : base + GROUP, pl.ds(at, CHUNK)] = low

    groups = rows // GROUP

    @pl.loop(0, chunks)
    def _(chunk):
        for group in range(1, groups - 1):
            raw_tile(group, chunk)

    for side in (0, 1):
        row = 7 if side == 0 else 8 + rows

        @pl.when(has[side])
        def _():
            edge_copy(1 - side).wait_recv()
            for level in range(levels):
                rim[level, row : row + 1, LANES : LANES + cols] = edge_in[
                    side, level : level + 1, :
                ]

        @pl.when(jnp.logical_not(has[side]))
        def _():
            for level in range(levels):
                rim[level, row : row + 1, LANES : LANES + cols] = jnp.zeros(
                    (1, cols), jnp.float32
                )

    for chunk in range(chunks):
        for group in (0, groups - 1):
            raw_tile(group, chunk)
        for side in (0, 1):
            @pl.when(has[side])
            def _():
                code_copy(side, chunk).start()

    inner = lax.broadcasted_iota(jnp.int32, (2 * WIDE, WIDE), 0)
    outer = lax.broadcasted_iota(jnp.int32, (2 * WIDE, WIDE), 1)
    high, low = halves(tap_at(inner - LANES - outer))
    bhigh[...] = high
    blow[...] = low
    outer = lax.broadcasted_iota(jnp.int32, (rows, 3 * rows), 0)
    inner = lax.broadcasted_iota(jnp.int32, (rows, 3 * rows), 1)
    high, low = halves(tap_at(inner - rows - outer))
    whigh[...] = high
    wboth[:rows] = high
    wboth[rows:] = low
    for side in (0, 1):
        base = 2 * rows * side

        @pl.when(jnp.logical_not(has[side]))
        def _():
            blank = jnp.zeros((2, rows, cols), jnp.bfloat16)
            dhigh[:, base : base + rows, :] = blank
            dlow[:, base : base + rows, :] = blank

    def product(a, b):
        return jnp.dot(a, b, preferred_element_type=jnp.float32)

    def zonal(block):
        at = block * WIDE
        high = mhigh[:, at : at + 2 * WIDE]
        low = mlow[:, at : at + 2 * WIDE]
        total = product(high, bhigh[...]) + product(high, blow[...]) + product(low, bhigh[...])
        out_ref[0, :, at : at + WIDE] = total[:rows]
        out_ref[1, :, at : at + WIDE] = total[rows:]

    done = 0
    for chunk in range(chunks):
        at = chunk * CHUNK
        for side in (0, 1):
            base = 2 * rows * side

            @pl.when(has[side])
            def _():
                code_copy(1 - side, chunk).wait_recv()
                for comp in (0, 1):
                    code = code_in[side, chunk, comp * rows : (comp + 1) * rows, :]
                    high, low = halves(decode(code))
                    dhigh[comp, base : base + rows, at : at + CHUNK] = high
                    dlow[comp, base : base + rows, at : at + CHUNK] = low

        for comp in (0, 1):
            both = product(wboth[...], dhigh[comp, :, at : at + CHUNK])
            rest = product(whigh[...], dlow[comp, :, at : at + CHUNK])
            high, low = halves(both[:rows] + (both[rows:] + rest))
            mhigh[comp * rows : (comp + 1) * rows, LANES + at : LANES + at + CHUNK] = high
            mlow[comp * rows : (comp + 1) * rows, LANES + at : LANES + at + CHUNK] = low
        ready = cols // WIDE if chunk == chunks - 1 else ((chunk + 1) * CHUNK - HALF) // WIDE
        for block in range(done, ready):
            zonal(block)
        done = ready

    for side in (0, 1):
        @pl.when(has[side])
        def _():
            edge_copy(side).wait_send()
            for chunk in range(chunks):
                code_copy(side, chunk).wait_send()


def solution(mesh):
    count = mesh.shape["row"]

    def body(innovation, background, level_weight):
        levels, rows, cols = innovation.shape
        assert rows == HALF and cols % CHUNK == 0
        chunks = cols // CHUNK
        f32, bf16 = jnp.float32, jnp.bfloat16

        def call(*args):
            return kernel(count, *args)

        return pl.pallas_call(
            call,
            out_shape=jax.ShapeDtypeStruct((2, rows, cols), f32),
            in_specs=[
                pl.BlockSpec(memory_space=pl.ANY),
                pl.BlockSpec(memory_space=pl.ANY),
                pl.BlockSpec(memory_space=pltpu.SMEM),
            ],
            out_specs=pl.BlockSpec(memory_space=pltpu.VMEM),
            scratch_shapes=[
                pltpu.VMEM((levels, rows, cols), bf16),
                pltpu.VMEM((levels, rows, cols), bf16),
                pltpu.VMEM((levels, rows + 16, cols + 2 * LANES), f32),
                pltpu.VMEM((2, levels, cols), f32),
                pltpu.VMEM((2, levels, cols), f32),
                pltpu.VMEM((chunks, 2 * rows, CHUNK), bf16),
                pltpu.VMEM((2, chunks, 2 * rows, CHUNK), bf16),
                pltpu.VMEM((2, 3 * rows, cols), bf16),
                pltpu.VMEM((2, 3 * rows, cols), bf16),
                pltpu.VMEM((2 * rows, cols + 2 * LANES), bf16),
                pltpu.VMEM((2 * rows, cols + 2 * LANES), bf16),
                pltpu.VMEM((rows, 3 * rows), bf16),
                pltpu.VMEM((2 * rows, 3 * rows), bf16),
                pltpu.VMEM((2 * WIDE, WIDE), bf16),
                pltpu.VMEM((2 * WIDE, WIDE), bf16),
                pltpu.SemaphoreType.DMA((2,)),
                pltpu.SemaphoreType.DMA((2,)),
                pltpu.SemaphoreType.DMA((2,)),
                pltpu.SemaphoreType.DMA((2, chunks)),
                pltpu.SemaphoreType.DMA((2, chunks)),
            ],
            compiler_params=pltpu.CompilerParams(
                collective_id=0, has_side_effects=True, vmem_limit_bytes=40 * 2**20
            ),
            name="align",
        )(innovation, background, level_weight)

    placed = (P("member", "row", None), P("member", "row", None), P())
    return jax.shard_map(
        body, mesh=mesh, in_specs=placed, out_specs=P("member", "row", None), check_vma=False
    )
```

```python
import jax
import jax.numpy as jnp
from jax import lax
from jax.experimental import pallas as pl
from jax.experimental.pallas import tpu as pltpu
from jax.sharding import PartitionSpec as P

HALF = 64
SIGMA = 64
LANES = 128
CHUNK = 512
GROUP = 16
WIDE = 256
SCALE = 4096.0


def tap_at(offset):
    grid = lax.broadcasted_iota(jnp.int32, (8, 2 * LANES), 1) - HALF
    off = grid.astype(jnp.float32)
    spread = jnp.float32(SIGMA)
    squares = jnp.where(grid <= HALF, jnp.exp(-off * off / (spread * spread)), 0.0)
    total = jnp.sqrt(jnp.sum(squares[:1], axis=1, keepdims=True))
    value = offset.astype(jnp.float32)
    value = jnp.exp(-value * value / (2.0 * spread * spread)) / total
    return jnp.where(jnp.abs(offset) <= HALF, value, 0.0)


def halves(value):
    high = value.astype(jnp.bfloat16)
    return high, (value - high.astype(jnp.float32)).astype(jnp.bfloat16)


def encode(raw):
    value = raw * SCALE
    value2 = value * value
    value4 = value2 * value2
    value8 = value4 * value4
    return jnp.where(value < 0.0, -value8, value8).astype(jnp.bfloat16)


def decode(code):
    code = code.astype(jnp.float32)
    size = jnp.exp2(jnp.log2(jnp.abs(code)) * 0.125) * (1.0 / SCALE)
    return jnp.where(code < 0.0, -size, size)


def kernel(
    count, inn_hbm, bg_hbm, lw_hbm, out_ref,
    lw_ref, inn, bg, rim, edge_out, edge_in, code_out, code_in, dhigh, dlow,
    mhigh, mlow, whigh, wboth, bhigh, blow,
    in_sem, edge_send, edge_recv, send_sem, recv_sem,
):
    levels, rows, cols = inn.shape
    chunks = cols // CHUNK
    phases = ((1, 2), (0, 3))
    me = lax.axis_index("row")
    has = (me > 0, me < count - 1)
    peer = (jnp.maximum(me - 1, 0), jnp.minimum(me + 1, count - 1))

    load_bg = pltpu.make_async_copy(bg_hbm, bg, in_sem.at[0])
    load_inn = pltpu.make_async_copy(inn_hbm, inn, in_sem.at[1])
    load_bg.start()
    load_inn.start()
    load_lw = pltpu.make_async_copy(lw_hbm, lw_ref, in_sem.at[2])
    load_lw.start()
    barrier = pltpu.get_barrier_semaphore()
    for side in (0, 1):
        @pl.when(has[side])
        def _():
            pl.semaphore_signal(
                barrier, inc=1, device_id={"row": peer[side]},
                device_id_type=pl.DeviceIdType.MESH,
            )

    zeros = jnp.zeros((levels, rows + 16, LANES), jnp.float32)
    rim[:, :, :LANES] = zeros
    rim[:, :, LANES + cols :] = zeros
    strip = jnp.zeros((2 * rows, LANES), jnp.bfloat16)
    for ref in (mhigh, mlow):
        ref[:, :LANES] = strip
        ref[:, LANES + cols :] = strip

    load_bg.wait()
    for level in range(levels):
        edge_out[0, level : level + 1, :] = bg[level, :16, :].astype(jnp.float32)[:1]
        edge_out[1, level : level + 1, :] = bg[level, rows - 16 :, :].astype(jnp.float32)[15:]
    pl.semaphore_wait(barrier, peer[1] - peer[0])

    def edge_copy(side):
        return pltpu.make_async_remote_copy(
            src_ref=edge_out.at[side], dst_ref=edge_in.at[1 - side],
            send_sem=edge_send.at[side], recv_sem=edge_recv.at[1 - side],
            device_id={"row": peer[side]}, device_id_type=pl.DeviceIdType.MESH,
        )

    def code_copy(side, phase, chunk):
        return pltpu.make_async_remote_copy(
            src_ref=code_out.at[phase, chunk], dst_ref=code_in.at[1 - side, phase, chunk],
            send_sem=send_sem.at[side, phase, chunk],
            recv_sem=recv_sem.at[1 - side, phase, chunk],
            device_id={"row": peer[side]}, device_id_type=pl.DeviceIdType.MESH,
        )

    for side in (0, 1):
        @pl.when(has[side])
        def _():
            edge_copy(side).start()

    @pl.loop(0, chunks)
    def _(chunk):
        at = pl.multiple_of(chunk * CHUNK, CHUNK)
        for level in range(levels):
            rim[level, 8 : 8 + rows, pl.ds(LANES + at, CHUNK)] = bg[
                level, :, pl.ds(at, CHUNK)
            ].astype(jnp.float32)

    load_inn.wait()
    load_lw.wait()

    def raw_tile(group, chunk):
        at = chunk * CHUNK
        top = 8 + group * GROUP
        wide = CHUNK + 2 * LANES
        numer_y = numer_x = None
        denom = jnp.ones((GROUP, CHUNK), jnp.float32)
        for level in range(levels):
            weight = lw_ref[level]
            line = rim[level, top : top + GROUP, pl.ds(at, wide)]
            left = pltpu.roll(line, 1, 1)[:, LANES : LANES + CHUNK]
            right = pltpu.roll(line, wide - 1, 1)[:, LANES : LANES + CHUNK]
            above = rim[level, top - 1 : top - 1 + GROUP, pl.ds(LANES + at, CHUNK)]
            below = rim[level, top + 1 : top + 1 + GROUP, pl.ds(LANES + at, CHUNK)]
            grad_x = 0.5 * (right - left)
            grad_y = 0.5 * (below - above)
            span = pl.ds(group * GROUP, GROUP)
            scaled = weight * inn[level, span, pl.ds(at, CHUNK)].astype(jnp.float32)
            part_y, part_x = scaled * grad_y, scaled * grad_x
            numer_y = part_y if numer_y is None else numer_y + part_y
            numer_x = part_x if numer_x is None else numer_x + part_x
            denom = denom + weight * (grad_y * grad_y + grad_x * grad_x)
        inverse = 1.0 / denom
        for comp, numer in enumerate((numer_y, numer_x)):
            raw = numer * inverse
            phase = phases.index([pair for pair in phases if group in pair][0])
            low_row = (2 * comp + phases[phase].index(group)) * GROUP
            code_out[phase, chunk, low_row : low_row + GROUP, :] = encode(raw)
            high, low = halves(raw)
            base = rows + group * GROUP
            dhigh[comp, base : base + GROUP, pl.ds(at, CHUNK)] = high
            dlow[comp, base : base + GROUP, pl.ds(at, CHUNK)] = low

    def send_phase(phase):
        for chunk in range(chunks):
            for group in phases[phase]:
                raw_tile(group, chunk)
            for side in (0, 1):
                @pl.when(has[side])
                def _():
                    code_copy(side, phase, chunk).start()

    send_phase(0)

    for side in (0, 1):
        row = 7 if side == 0 else 8 + rows

        @pl.when(has[side])
        def _():
            edge_copy(1 - side).wait_recv()
            for level in range(levels):
                rim[level, row : row + 1, LANES : LANES + cols] = edge_in[
                    side, level : level + 1, :
                ]

        @pl.when(jnp.logical_not(has[side]))
        def _():
            for level in range(levels):
                rim[level, row : row + 1, LANES : LANES + cols] = jnp.zeros(
                    (1, cols), jnp.float32
                )

    send_phase(1)

    inner = lax.broadcasted_iota(jnp.int32, (2 * WIDE, WIDE), 0)
    outer = lax.broadcasted_iota(jnp.int32, (2 * WIDE, WIDE), 1)
    high, low = halves(tap_at(inner - LANES - outer))
    bhigh[...] = high
    blow[...] = low
    outer = lax.broadcasted_iota(jnp.int32, (rows, 3 * rows), 0)
    inner = lax.broadcasted_iota(jnp.int32, (rows, 3 * rows), 1)
    high, low = halves(tap_at(inner - rows - outer))
    whigh[...] = high
    wboth[:rows] = high
    wboth[rows:] = low
    for side in (0, 1):
        base = 2 * rows * side

        @pl.when(jnp.logical_not(has[side]))
        def _():
            blank = jnp.zeros((2, rows, cols), jnp.bfloat16)
            dhigh[:, base : base + rows, :] = blank
            dlow[:, base : base + rows, :] = blank

    def product(a, b):
        return jnp.dot(a, b, preferred_element_type=jnp.float32)

    def zonal(block):
        at = block * WIDE
        high = mhigh[:, at : at + 2 * WIDE]
        low = mlow[:, at : at + 2 * WIDE]
        total = product(high, bhigh[...]) + product(high, blow[...]) + product(low, bhigh[...])
        out_ref[0, :, at : at + WIDE] = total[:rows]
        out_ref[1, :, at : at + WIDE] = total[rows:]

    def receive(phase, chunk):
        at = chunk * CHUNK
        for side in (0, 1):
            @pl.when(has[side])
            def _():
                code_copy(1 - side, phase, chunk).wait_recv()
                for comp in (0, 1):
                    for order, group in enumerate(phases[phase]):
                        low_row = (2 * comp + order) * GROUP
                        code = code_in[side, phase, chunk, low_row : low_row + GROUP, :]
                        high, low = halves(decode(code))
                        base = 2 * rows * side + group * GROUP
                        dhigh[comp, base : base + GROUP, at : at + CHUNK] = high
                        dlow[comp, base : base + GROUP, at : at + CHUNK] = low

    for chunk in range(chunks):
        receive(0, chunk)
    done = 0
    for chunk in range(chunks):
        at = chunk * CHUNK
        receive(1, chunk)

        for comp in (0, 1):
            both = product(wboth[...], dhigh[comp, :, at : at + CHUNK])
            rest = product(whigh[...], dlow[comp, :, at : at + CHUNK])
            high, low = halves(both[:rows] + (both[rows:] + rest))
            mhigh[comp * rows : (comp + 1) * rows, LANES + at : LANES + at + CHUNK] = high
            mlow[comp * rows : (comp + 1) * rows, LANES + at : LANES + at + CHUNK] = low
        ready = cols // WIDE if chunk == chunks - 1 else ((chunk + 1) * CHUNK - HALF) // WIDE
        for block in range(done, ready):
            zonal(block)
        done = ready

    for side in (0, 1):
        @pl.when(has[side])
        def _():
            edge_copy(side).wait_send()
            for phase in (0, 1):
                for chunk in range(chunks):
                    code_copy(side, phase, chunk).wait_send()


def solution(mesh):
    count = mesh.shape["row"]

    def body(innovation, background, level_weight):
        levels, rows, cols = innovation.shape
        assert rows == HALF and cols % CHUNK == 0
        chunks = cols // CHUNK
        f32, bf16 = jnp.float32, jnp.bfloat16

        def call(*args):
            return kernel(count, *args)

        return pl.pallas_call(
            call,
            out_shape=jax.ShapeDtypeStruct((2, rows, cols), f32),
            in_specs=[
                pl.BlockSpec(memory_space=pltpu.HBM),
                pl.BlockSpec(memory_space=pltpu.HBM),
                pl.BlockSpec(memory_space=pltpu.HBM),
            ],
            out_specs=pl.BlockSpec(memory_space=pltpu.VMEM),
            scratch_shapes=[
                pltpu.SMEM((levels,), f32),
                pltpu.VMEM((levels, rows, cols), bf16),
                pltpu.VMEM((levels, rows, cols), bf16),
                pltpu.VMEM((levels, rows + 16, cols + 2 * LANES), f32),
                pltpu.VMEM((2, levels, cols), f32),
                pltpu.VMEM((2, levels, cols), f32),
                pltpu.VMEM((2, chunks, rows, CHUNK), bf16),
                pltpu.VMEM((2, 2, chunks, rows, CHUNK), bf16),
                pltpu.VMEM((2, 3 * rows, cols), bf16),
                pltpu.VMEM((2, 3 * rows, cols), bf16),
                pltpu.VMEM((2 * rows, cols + 2 * LANES), bf16),
                pltpu.VMEM((2 * rows, cols + 2 * LANES), bf16),
                pltpu.VMEM((rows, 3 * rows), bf16),
                pltpu.VMEM((2 * rows, 3 * rows), bf16),
                pltpu.VMEM((2 * WIDE, WIDE), bf16),
                pltpu.VMEM((2 * WIDE, WIDE), bf16),
                pltpu.SemaphoreType.DMA((3,)),
                pltpu.SemaphoreType.DMA((2,)),
                pltpu.SemaphoreType.DMA((2,)),
                pltpu.SemaphoreType.DMA((2, 2, chunks)),
                pltpu.SemaphoreType.DMA((2, 2, chunks)),
            ],
            compiler_params=pltpu.CompilerParams(
                collective_id=0, has_side_effects=True, vmem_limit_bytes=40 * 2**20
            ),
            name="align",
        )(*(pltpu.with_memory_space_constraint(v, pltpu.HBM) for v in (innovation, background, level_weight)))

    placed = (P("member", "row", None), P("member", "row", None), P())
    return jax.shard_map(
        body, mesh=mesh, in_specs=placed, out_specs=P("member", "row", None), check_vma=False
    )
```

```python
import jax
import jax.numpy as jnp
from jax import lax
from jax.experimental import pallas as pl
from jax.experimental.pallas import tpu as pltpu
from jax.sharding import PartitionSpec as P

HALF = 64
SIGMA = 64
LANES = 128
CHUNK = 512
GROUP = 16
WIDE = 256
SCALE = 4096.0


def tap_at(offset):
    grid = lax.broadcasted_iota(jnp.int32, (8, 2 * LANES), 1) - HALF
    off = grid.astype(jnp.float32)
    spread = jnp.float32(SIGMA)
    squares = jnp.where(grid <= HALF, jnp.exp(-off * off / (spread * spread)), 0.0)
    total = jnp.sqrt(jnp.sum(squares[:1], axis=1, keepdims=True))
    value = offset.astype(jnp.float32)
    value = jnp.exp(-value * value / (2.0 * spread * spread)) / total
    return jnp.where(jnp.abs(offset) <= HALF, value, 0.0)


def halves(value):
    high = value.astype(jnp.bfloat16)
    return high, (value - high.astype(jnp.float32)).astype(jnp.bfloat16)


def encode(raw):
    value = raw * SCALE
    value2 = value * value
    value4 = value2 * value2
    value8 = value4 * value4
    return jnp.where(value < 0.0, -value8, value8).astype(jnp.bfloat16)


def decode(code):
    code = code.astype(jnp.float32)
    size = jnp.exp2(jnp.log2(jnp.abs(code)) * 0.125) * (1.0 / SCALE)
    return jnp.where(code < 0.0, -size, size)


def kernel(
    count, inn_hbm, bg_hbm, lw_hbm, out_ref,
    lw_ref, inn, bg, rim, edge_out, edge_in, code_out, code_in, dhigh, dlow,
    mhigh, mlow, whigh, wboth, bhigh, blow,
    relay, in_sem, edge_send, edge_recv, send_sem, recv_sem, relay_recv, relay_send,
):
    levels, rows, cols = inn.shape
    chunks = cols // CHUNK
    phases = ((1, 2), (0, 3))
    me = lax.axis_index("row")
    has = (me > 0, me < count - 1)
    peer = (jnp.maximum(me - 1, 0), jnp.minimum(me + 1, count - 1))

    blocks = count // 4 if count % 4 == 0 else 0
    pieces = 2 * chunks
    place = lax.rem(me, 4)
    where = lax.div(me, 4)
    if blocks:
        share = (where * pieces // blocks, (blocks - 1 - where) * pieces // blocks)
    starts = (place == 0, place == 3)
    passes = (place == 3, place == 0)
    partner = jnp.where(place == 0, me + 3, me - 3)
    corner = starts[0] | starts[1]
    onward = (me - 4, me + 4)

    load_bg = pltpu.make_async_copy(bg_hbm, bg, in_sem.at[0])
    load_inn = pltpu.make_async_copy(inn_hbm, inn, in_sem.at[1])
    load_bg.start()
    load_inn.start()
    load_lw = pltpu.make_async_copy(lw_hbm, lw_ref, in_sem.at[2])
    load_lw.start()
    barrier = pltpu.get_barrier_semaphore()
    for side in (0, 1):
        @pl.when(has[side])
        def _():
            pl.semaphore_signal(
                barrier, inc=1, device_id={"row": peer[side]},
                device_id_type=pl.DeviceIdType.MESH,
            )

    others = (
        (corner, partner), (corner & (where > 0), onward[0]),
        (corner & (where < blocks - 1), onward[1]),
    )
    for test, other in others if blocks else ():
        @pl.when(test)
        def _():
            pl.semaphore_signal(
                barrier, inc=1, device_id={"row": other},
                device_id_type=pl.DeviceIdType.MESH,
            )

    zeros = jnp.zeros((levels, rows + 16, LANES), jnp.float32)
    rim[:, :, :LANES] = zeros
    rim[:, :, LANES + cols :] = zeros
    strip = jnp.zeros((2 * rows, LANES), jnp.bfloat16)
    for ref in (mhigh, mlow):
        ref[:, :LANES] = strip
        ref[:, LANES + cols :] = strip

    load_bg.wait()
    for level in range(levels):
        edge_out[0, level : level + 1, :] = bg[level, :16, :].astype(jnp.float32)[:1]
        edge_out[1, level : level + 1, :] = bg[level, rows - 16 :, :].astype(jnp.float32)[15:]
    greeted = peer[1] - peer[0]
    if blocks:
        greeted = greeted + sum(jnp.where(test, 1, 0) for test, _ in others)
    pl.semaphore_wait(barrier, greeted)

    def edge_copy(side):
        return pltpu.make_async_remote_copy(
            src_ref=edge_out.at[side], dst_ref=edge_in.at[1 - side],
            send_sem=edge_send.at[side], recv_sem=edge_recv.at[1 - side],
            device_id={"row": peer[side]}, device_id_type=pl.DeviceIdType.MESH,
        )

    def code_copy(side, phase, chunk):
        return pltpu.make_async_remote_copy(
            src_ref=code_out.at[phase, chunk], dst_ref=code_in.at[1 - side, phase, chunk],
            send_sem=send_sem.at[side, phase, chunk],
            recv_sem=recv_sem.at[1 - side, phase, chunk],
            device_id={"row": peer[side]}, device_id_type=pl.DeviceIdType.MESH,
        )

    def relay_copy(side, phase, chunk):
        piece = phase * chunks + chunk
        return pltpu.make_async_remote_copy(
            src_ref=code_out.at[phase, chunk], dst_ref=relay.at[piece],
            send_sem=send_sem.at[side, phase, chunk], recv_sem=relay_recv.at[piece],
            device_id={"row": partner}, device_id_type=pl.DeviceIdType.MESH,
        )

    def onward_copy(side, phase, chunk):
        piece = phase * chunks + chunk
        return pltpu.make_async_remote_copy(
            src_ref=relay.at[piece], dst_ref=code_in.at[1 - side, phase, chunk],
            send_sem=relay_send.at[piece], recv_sem=recv_sem.at[1 - side, phase, chunk],
            device_id={"row": onward[side]}, device_id_type=pl.DeviceIdType.MESH,
        )

    def start_code(side, phase, chunk):
        if not blocks:
            @pl.when(has[side])
            def _():
                code_copy(side, phase, chunk).start()
            return
        indirect = starts[side] & (phase * chunks + chunk < share[side])

        @pl.when(indirect)
        def _():
            relay_copy(side, phase, chunk).start()

        @pl.when(has[side] & jnp.logical_not(indirect))
        def _():
            code_copy(side, phase, chunk).start()

    def pass_on(phase):
        for chunk in range(chunks if blocks else 0):
            for side in (0, 1):
                @pl.when(passes[side] & (phase * chunks + chunk < share[side]))
                def _():
                    relay_copy(side, phase, chunk).wait_recv()
                    onward_copy(side, phase, chunk).start()

    for side in (0, 1):
        @pl.when(has[side])
        def _():
            edge_copy(side).start()

    @pl.loop(0, chunks)
    def _(chunk):
        at = pl.multiple_of(chunk * CHUNK, CHUNK)
        for level in range(levels):
            rim[level, 8 : 8 + rows, pl.ds(LANES + at, CHUNK)] = bg[
                level, :, pl.ds(at, CHUNK)
            ].astype(jnp.float32)

    load_inn.wait()
    load_lw.wait()

    def raw_tile(group, chunk):
        at = chunk * CHUNK
        top = 8 + group * GROUP
        wide = CHUNK + 2 * LANES
        numer_y = numer_x = None
        denom = jnp.ones((GROUP, CHUNK), jnp.float32)
        for level in range(levels):
            weight = lw_ref[level]
            line = rim[level, top : top + GROUP, pl.ds(at, wide)]
            left = pltpu.roll(line, 1, 1)[:, LANES : LANES + CHUNK]
            right = pltpu.roll(line, wide - 1, 1)[:, LANES : LANES + CHUNK]
            above = rim[level, top - 1 : top - 1 + GROUP, pl.ds(LANES + at, CHUNK)]
            below = rim[level, top + 1 : top + 1 + GROUP, pl.ds(LANES + at, CHUNK)]
            grad_x = 0.5 * (right - left)
            grad_y = 0.5 * (below - above)
            span = pl.ds(group * GROUP, GROUP)
            scaled = weight * inn[level, span, pl.ds(at, CHUNK)].astype(jnp.float32)
            part_y, part_x = scaled * grad_y, scaled * grad_x
            numer_y = part_y if numer_y is None else numer_y + part_y
            numer_x = part_x if numer_x is None else numer_x + part_x
            denom = denom + weight * (grad_y * grad_y + grad_x * grad_x)
        inverse = 1.0 / denom
        for comp, numer in enumerate((numer_y, numer_x)):
            raw = numer * inverse
            phase = phases.index([pair for pair in phases if group in pair][0])
            low_row = (2 * comp + phases[phase].index(group)) * GROUP
            code_out[phase, chunk, low_row : low_row + GROUP, :] = encode(raw)
            high, low = halves(raw)
            base = rows + group * GROUP
            dhigh[comp, base : base + GROUP, pl.ds(at, CHUNK)] = high
            dlow[comp, base : base + GROUP, pl.ds(at, CHUNK)] = low

    def send_phase(phase):
        for chunk in range(chunks):
            for group in phases[phase]:
                raw_tile(group, chunk)
            for side in (0, 1):
                start_code(side, phase, chunk)

    send_phase(0)

    for side in (0, 1):
        row = 7 if side == 0 else 8 + rows

        @pl.when(has[side])
        def _():
            edge_copy(1 - side).wait_recv()
            for level in range(levels):
                rim[level, row : row + 1, LANES : LANES + cols] = edge_in[
                    side, level : level + 1, :
                ]

        @pl.when(jnp.logical_not(has[side]))
        def _():
            for level in range(levels):
                rim[level, row : row + 1, LANES : LANES + cols] = jnp.zeros(
                    (1, cols), jnp.float32
                )

    send_phase(1)

    inner = lax.broadcasted_iota(jnp.int32, (2 * WIDE, WIDE), 0)
    outer = lax.broadcasted_iota(jnp.int32, (2 * WIDE, WIDE), 1)
    high, low = halves(tap_at(inner - LANES - outer))
    bhigh[...] = high
    blow[...] = low
    outer = lax.broadcasted_iota(jnp.int32, (rows, 3 * rows), 0)
    inner = lax.broadcasted_iota(jnp.int32, (rows, 3 * rows), 1)
    high, low = halves(tap_at(inner - rows - outer))
    whigh[...] = high
    wboth[:rows] = high
    wboth[rows:] = low
    for side in (0, 1):
        base = 2 * rows * side

        @pl.when(jnp.logical_not(has[side]))
        def _():
            blank = jnp.zeros((2, rows, cols), jnp.bfloat16)
            dhigh[:, base : base + rows, :] = blank
            dlow[:, base : base + rows, :] = blank

    def product(a, b):
        return jnp.dot(a, b, preferred_element_type=jnp.float32)

    def zonal(block):
        at = block * WIDE
        high = mhigh[:, at : at + 2 * WIDE]
        low = mlow[:, at : at + 2 * WIDE]
        total = product(high, bhigh[...]) + product(high, blow[...]) + product(low, bhigh[...])
        out_ref[0, :, at : at + WIDE] = total[:rows]
        out_ref[1, :, at : at + WIDE] = total[rows:]

    def receive(phase, chunk):
        at = chunk * CHUNK
        for side in (0, 1):
            @pl.when(has[side])
            def _():
                code_copy(1 - side, phase, chunk).wait_recv()
                for comp in (0, 1):
                    for order, group in enumerate(phases[phase]):
                        low_row = (2 * comp + order) * GROUP
                        code = code_in[side, phase, chunk, low_row : low_row + GROUP, :]
                        high, low = halves(decode(code))
                        base = 2 * rows * side + group * GROUP
                        dhigh[comp, base : base + GROUP, at : at + CHUNK] = high
                        dlow[comp, base : base + GROUP, at : at + CHUNK] = low

    pass_on(0)
    for chunk in range(chunks):
        receive(0, chunk)
    pass_on(1)
    done = 0
    for chunk in range(chunks):
        at = chunk * CHUNK
        receive(1, chunk)

        for comp in (0, 1):
            both = product(wboth[...], dhigh[comp, :, at : at + CHUNK])
            rest = product(whigh[...], dlow[comp, :, at : at + CHUNK])
            high, low = halves(both[:rows] + (both[rows:] + rest))
            mhigh[comp * rows : (comp + 1) * rows, LANES + at : LANES + at + CHUNK] = high
            mlow[comp * rows : (comp + 1) * rows, LANES + at : LANES + at + CHUNK] = low
        ready = cols // WIDE if chunk == chunks - 1 else ((chunk + 1) * CHUNK - HALF) // WIDE
        for block in range(done, ready):
            zonal(block)
        done = ready

    for side in (0, 1):
        @pl.when(has[side])
        def _():
            edge_copy(side).wait_send()
            for phase in (0, 1):
                for chunk in range(chunks):
                    code_copy(side, phase, chunk).wait_send()

    for side in (0, 1):
        for phase in (0, 1):
            for chunk in range(chunks if blocks else 0):
                @pl.when(passes[side] & (phase * chunks + chunk < share[side]))
                def _():
                    onward_copy(side, phase, chunk).wait_send()


def solution(mesh):
    count = mesh.shape["row"]

    def body(innovation, background, level_weight):
        levels, rows, cols = innovation.shape
        assert rows == HALF and cols % CHUNK == 0
        chunks = cols // CHUNK
        f32, bf16 = jnp.float32, jnp.bfloat16

        def call(*args):
            return kernel(count, *args)

        return pl.pallas_call(
            call,
            out_shape=jax.ShapeDtypeStruct((2, rows, cols), f32),
            in_specs=[
                pl.BlockSpec(memory_space=pltpu.HBM),
                pl.BlockSpec(memory_space=pltpu.HBM),
                pl.BlockSpec(memory_space=pltpu.HBM),
            ],
            out_specs=pl.BlockSpec(memory_space=pltpu.VMEM),
            scratch_shapes=[
                pltpu.SMEM((levels,), f32),
                pltpu.VMEM((levels, rows, cols), bf16),
                pltpu.VMEM((levels, rows, cols), bf16),
                pltpu.VMEM((levels, rows + 16, cols + 2 * LANES), f32),
                pltpu.VMEM((2, levels, cols), f32),
                pltpu.VMEM((2, levels, cols), f32),
                pltpu.VMEM((2, chunks, rows, CHUNK), bf16),
                pltpu.VMEM((2, 2, chunks, rows, CHUNK), bf16),
                pltpu.VMEM((2, 3 * rows, cols), bf16),
                pltpu.VMEM((2, 3 * rows, cols), bf16),
                pltpu.VMEM((2 * rows, cols + 2 * LANES), bf16),
                pltpu.VMEM((2 * rows, cols + 2 * LANES), bf16),
                pltpu.VMEM((rows, 3 * rows), bf16),
                pltpu.VMEM((2 * rows, 3 * rows), bf16),
                pltpu.VMEM((2 * WIDE, WIDE), bf16),
                pltpu.VMEM((2 * WIDE, WIDE), bf16),
                pltpu.VMEM((2 * chunks, rows, CHUNK), bf16),
                pltpu.SemaphoreType.DMA((3,)),
                pltpu.SemaphoreType.DMA((2,)),
                pltpu.SemaphoreType.DMA((2,)),
                pltpu.SemaphoreType.DMA((2, 2, chunks)),
                pltpu.SemaphoreType.DMA((2, 2, chunks)),
                pltpu.SemaphoreType.DMA((2 * chunks,)),
                pltpu.SemaphoreType.DMA((2 * chunks,)),
            ],
            compiler_params=pltpu.CompilerParams(
                collective_id=0, has_side_effects=True, vmem_limit_bytes=40 * 2**20
            ),
            name="align",
        )(*(pltpu.with_memory_space_constraint(v, pltpu.HBM) for v in (innovation, background, level_weight)))

    placed = (P("member", "row", None), P("member", "row", None), P())
    return jax.shard_map(
        body, mesh=mesh, in_specs=placed, out_specs=P("member", "row", None), check_vma=False
    )
```

```python
import jax
import jax.numpy as jnp
from jax import lax
from jax.experimental import pallas as pl
from jax.experimental.pallas import tpu as pltpu
from jax.sharding import PartitionSpec as P

HALF = 64
SIGMA = 64
LANES = 128
CHUNK = 512
GROUP = 16
WIDE = 256
SCALE = 4096.0


def tap_at(offset):
    grid = lax.broadcasted_iota(jnp.int32, (8, 2 * LANES), 1) - HALF
    off = grid.astype(jnp.float32)
    spread = jnp.float32(SIGMA)
    squares = jnp.where(grid <= HALF, jnp.exp(-off * off / (spread * spread)), 0.0)
    total = jnp.sqrt(jnp.sum(squares[:1], axis=1, keepdims=True))
    value = offset.astype(jnp.float32)
    value = jnp.exp(-value * value / (2.0 * spread * spread)) / total
    return jnp.where(jnp.abs(offset) <= HALF, value, 0.0)


def halves(value):
    high = value.astype(jnp.bfloat16)
    return high, (value - high.astype(jnp.float32)).astype(jnp.bfloat16)


def encode(raw):
    value = raw * SCALE
    value2 = value * value
    value4 = value2 * value2
    value8 = value4 * value4
    return jnp.where(value < 0.0, -value8, value8).astype(jnp.bfloat16)


def decode(code):
    code = code.astype(jnp.float32)
    size = jnp.exp2(jnp.log2(jnp.abs(code)) * 0.125) * (1.0 / SCALE)
    return jnp.where(code < 0.0, -size, size)


def kernel(
    count, inn_hbm, bg_hbm, lw_hbm, out_ref,
    lw_ref, inn, bg, rim, edge_out, edge_in, code_out, code_in, dhigh, dlow,
    mhigh, mlow, whigh, wboth, bhigh, blow,
    relay, in_sem, edge_send, edge_recv, send_sem, recv_sem, relay_recv, relay_send,
):
    levels, rows, cols = inn.shape
    chunks = cols // CHUNK
    phases = ((1, 2), (0, 3))
    me = lax.axis_index("row")
    has = (me > 0, me < count - 1)
    peer = (jnp.maximum(me - 1, 0), jnp.minimum(me + 1, count - 1))

    blocks = count // 4 if count % 4 == 0 else 0
    place = lax.rem(me, 4)
    where = lax.div(me, 4)
    if blocks:
        share = (where * chunks // blocks, (blocks - 1 - where) * chunks // blocks)
    starts = (place == 0, place == 3)
    passes = (place == 3, place == 0)
    partner = jnp.where(place == 0, me + 3, me - 3)
    corner = starts[0] | starts[1]
    onward = (me - 4, me + 4)

    load_bg = pltpu.make_async_copy(bg_hbm, bg, in_sem.at[0])
    load_inn = pltpu.make_async_copy(inn_hbm, inn, in_sem.at[1])
    load_bg.start()
    load_inn.start()
    load_lw = pltpu.make_async_copy(lw_hbm, lw_ref, in_sem.at[2])
    load_lw.start()
    barrier = pltpu.get_barrier_semaphore()
    for side in (0, 1):
        @pl.when(has[side])
        def _():
            pl.semaphore_signal(
                barrier, inc=1, device_id={"row": peer[side]},
                device_id_type=pl.DeviceIdType.MESH,
            )

    others = (
        (corner, partner), (corner & (where > 0), onward[0]),
        (corner & (where < blocks - 1), onward[1]),
    )
    for test, other in others if blocks else ():
        @pl.when(test)
        def _():
            pl.semaphore_signal(
                barrier, inc=1, device_id={"row": other},
                device_id_type=pl.DeviceIdType.MESH,
            )

    zeros = jnp.zeros((levels, rows + 16, LANES), jnp.float32)
    rim[:, :, :LANES] = zeros
    rim[:, :, LANES + cols :] = zeros
    strip = jnp.zeros((2 * rows, LANES), jnp.bfloat16)
    for ref in (mhigh, mlow):
        ref[:, :LANES] = strip
        ref[:, LANES + cols :] = strip

    load_bg.wait()
    for level in range(levels):
        edge_out[0, level : level + 1, :] = bg[level, :16, :].astype(jnp.float32)[:1]
        edge_out[1, level : level + 1, :] = bg[level, rows - 16 :, :].astype(jnp.float32)[15:]
    greeted = peer[1] - peer[0]
    if blocks:
        greeted = greeted + sum(jnp.where(test, 1, 0) for test, _ in others)
    pl.semaphore_wait(barrier, greeted)

    def edge_copy(side):
        return pltpu.make_async_remote_copy(
            src_ref=edge_out.at[side], dst_ref=edge_in.at[1 - side],
            send_sem=edge_send.at[side], recv_sem=edge_recv.at[1 - side],
            device_id={"row": peer[side]}, device_id_type=pl.DeviceIdType.MESH,
        )

    def code_copy(side, phase, chunk):
        return pltpu.make_async_remote_copy(
            src_ref=code_out.at[phase, chunk], dst_ref=code_in.at[1 - side, phase, chunk],
            send_sem=send_sem.at[side, phase, chunk],
            recv_sem=recv_sem.at[1 - side, phase, chunk],
            device_id={"row": peer[side]}, device_id_type=pl.DeviceIdType.MESH,
        )

    def relay_copy(side, phase, chunk):
        piece = phase * chunks + chunk
        return pltpu.make_async_remote_copy(
            src_ref=code_out.at[phase, chunk], dst_ref=relay.at[piece],
            send_sem=send_sem.at[side, phase, chunk], recv_sem=relay_recv.at[piece],
            device_id={"row": partner}, device_id_type=pl.DeviceIdType.MESH,
        )

    def onward_copy(side, phase, chunk):
        piece = phase * chunks + chunk
        return pltpu.make_async_remote_copy(
            src_ref=relay.at[piece], dst_ref=code_in.at[1 - side, phase, chunk],
            send_sem=relay_send.at[piece], recv_sem=recv_sem.at[1 - side, phase, chunk],
            device_id={"row": onward[side]}, device_id_type=pl.DeviceIdType.MESH,
        )

    def start_code(side, phase, chunk):
        if phase == 1 or not blocks:
            @pl.when(has[side])
            def _():
                code_copy(side, phase, chunk).start()
            return
        indirect = starts[side] & (phase * chunks + chunk < share[side])

        @pl.when(indirect)
        def _():
            relay_copy(side, phase, chunk).start()

        @pl.when(has[side] & jnp.logical_not(indirect))
        def _():
            code_copy(side, phase, chunk).start()

    def pass_on(phase):
        for chunk in range(chunks if blocks else 0):
            for side in (0, 1):
                @pl.when(passes[side] & (phase * chunks + chunk < share[side]))
                def _():
                    relay_copy(side, phase, chunk).wait_recv()
                    onward_copy(side, phase, chunk).start()

    for side in (0, 1):
        @pl.when(has[side])
        def _():
            edge_copy(side).start()

    @pl.loop(0, chunks)
    def _(chunk):
        at = pl.multiple_of(chunk * CHUNK, CHUNK)
        for level in range(levels):
            rim[level, 8 : 8 + rows, pl.ds(LANES + at, CHUNK)] = bg[
                level, :, pl.ds(at, CHUNK)
            ].astype(jnp.float32)

    load_inn.wait()
    load_lw.wait()

    def raw_tile(group, chunk):
        at = chunk * CHUNK
        top = 8 + group * GROUP
        wide = CHUNK + 2 * LANES
        numer_y = numer_x = None
        denom = jnp.ones((GROUP, CHUNK), jnp.float32)
        for level in range(levels):
            weight = lw_ref[level]
            line = rim[level, top : top + GROUP, pl.ds(at, wide)]
            left = pltpu.roll(line, 1, 1)[:, LANES : LANES + CHUNK]
            right = pltpu.roll(line, wide - 1, 1)[:, LANES : LANES + CHUNK]
            above = rim[level, top - 1 : top - 1 + GROUP, pl.ds(LANES + at, CHUNK)]
            below = rim[level, top + 1 : top + 1 + GROUP, pl.ds(LANES + at, CHUNK)]
            grad_x = 0.5 * (right - left)
            grad_y = 0.5 * (below - above)
            span = pl.ds(group * GROUP, GROUP)
            scaled = weight * inn[level, span, pl.ds(at, CHUNK)].astype(jnp.float32)
            part_y, part_x = scaled * grad_y, scaled * grad_x
            numer_y = part_y if numer_y is None else numer_y + part_y
            numer_x = part_x if numer_x is None else numer_x + part_x
            denom = denom + weight * (grad_y * grad_y + grad_x * grad_x)
        inverse = 1.0 / denom
        for comp, numer in enumerate((numer_y, numer_x)):
            raw = numer * inverse
            phase = phases.index([pair for pair in phases if group in pair][0])
            low_row = (2 * comp + phases[phase].index(group)) * GROUP
            code_out[phase, chunk, low_row : low_row + GROUP, :] = encode(raw)
            high, low = halves(raw)
            base = rows + group * GROUP
            dhigh[comp, base : base + GROUP, pl.ds(at, CHUNK)] = high
            dlow[comp, base : base + GROUP, pl.ds(at, CHUNK)] = low

    def send_phase(phase):
        for chunk in range(chunks):
            for group in phases[phase]:
                raw_tile(group, chunk)
            for side in (0, 1):
                start_code(side, phase, chunk)

    send_phase(0)

    for side in (0, 1):
        row = 7 if side == 0 else 8 + rows

        @pl.when(has[side])
        def _():
            edge_copy(1 - side).wait_recv()
            for level in range(levels):
                rim[level, row : row + 1, LANES : LANES + cols] = edge_in[
                    side, level : level + 1, :
                ]

        @pl.when(jnp.logical_not(has[side]))
        def _():
            for level in range(levels):
                rim[level, row : row + 1, LANES : LANES + cols] = jnp.zeros(
                    (1, cols), jnp.float32
                )

    send_phase(1)

    inner = lax.broadcasted_iota(jnp.int32, (2 * WIDE, WIDE), 0)
    outer = lax.broadcasted_iota(jnp.int32, (2 * WIDE, WIDE), 1)
    high, low = halves(tap_at(inner - LANES - outer))
    bhigh[...] = high
    blow[...] = low
    outer = lax.broadcasted_iota(jnp.int32, (rows, 3 * rows), 0)
    inner = lax.broadcasted_iota(jnp.int32, (rows, 3 * rows), 1)
    high, low = halves(tap_at(inner - rows - outer))
    whigh[...] = high
    wboth[:rows] = high
    wboth[rows:] = low
    for side in (0, 1):
        base = 2 * rows * side

        @pl.when(jnp.logical_not(has[side]))
        def _():
            blank = jnp.zeros((2, rows, cols), jnp.bfloat16)
            dhigh[:, base : base + rows, :] = blank
            dlow[:, base : base + rows, :] = blank

    def product(a, b):
        return jnp.dot(a, b, preferred_element_type=jnp.float32)

    def zonal(block):
        at = block * WIDE
        high = mhigh[:, at : at + 2 * WIDE]
        low = mlow[:, at : at + 2 * WIDE]
        total = product(high, bhigh[...]) + product(high, blow[...]) + product(low, bhigh[...])
        out_ref[0, :, at : at + WIDE] = total[:rows]
        out_ref[1, :, at : at + WIDE] = total[rows:]

    def receive(phase, chunk):
        at = chunk * CHUNK
        for side in (0, 1):
            @pl.when(has[side])
            def _():
                code_copy(1 - side, phase, chunk).wait_recv()
                for comp in (0, 1):
                    for order, group in enumerate(phases[phase]):
                        low_row = (2 * comp + order) * GROUP
                        code = code_in[side, phase, chunk, low_row : low_row + GROUP, :]
                        high, low = halves(decode(code))
                        base = 2 * rows * side + group * GROUP
                        dhigh[comp, base : base + GROUP, at : at + CHUNK] = high
                        dlow[comp, base : base + GROUP, at : at + CHUNK] = low

    pass_on(0)
    for chunk in range(chunks):
        receive(0, chunk)
    done = 0
    for chunk in range(chunks):
        at = chunk * CHUNK
        receive(1, chunk)

        for comp in (0, 1):
            both = product(wboth[...], dhigh[comp, :, at : at + CHUNK])
            rest = product(whigh[...], dlow[comp, :, at : at + CHUNK])
            high, low = halves(both[:rows] + (both[rows:] + rest))
            mhigh[comp * rows : (comp + 1) * rows, LANES + at : LANES + at + CHUNK] = high
            mlow[comp * rows : (comp + 1) * rows, LANES + at : LANES + at + CHUNK] = low
        ready = cols // WIDE if chunk == chunks - 1 else ((chunk + 1) * CHUNK - HALF) // WIDE
        for block in range(done, ready):
            zonal(block)
        done = ready

    for side in (0, 1):
        @pl.when(has[side])
        def _():
            edge_copy(side).wait_send()
            for phase in (0, 1):
                for chunk in range(chunks):
                    code_copy(side, phase, chunk).wait_send()

    for side in (0, 1):
        for chunk in range(chunks if blocks else 0):
            @pl.when(passes[side] & (chunk < share[side]))
            def _():
                onward_copy(side, 0, chunk).wait_send()


def solution(mesh):
    count = mesh.shape["row"]

    def body(innovation, background, level_weight):
        levels, rows, cols = innovation.shape
        assert rows == HALF and cols % CHUNK == 0
        chunks = cols // CHUNK
        f32, bf16 = jnp.float32, jnp.bfloat16

        def call(*args):
            return kernel(count, *args)

        return pl.pallas_call(
            call,
            out_shape=jax.ShapeDtypeStruct((2, rows, cols), f32),
            in_specs=[
                pl.BlockSpec(memory_space=pltpu.HBM),
                pl.BlockSpec(memory_space=pltpu.HBM),
                pl.BlockSpec(memory_space=pltpu.HBM),
            ],
            out_specs=pl.BlockSpec(memory_space=pltpu.VMEM),
            scratch_shapes=[
                pltpu.SMEM((levels,), f32),
                pltpu.VMEM((levels, rows, cols), bf16),
                pltpu.VMEM((levels, rows, cols), bf16),
                pltpu.VMEM((levels, rows + 16, cols + 2 * LANES), f32),
                pltpu.VMEM((2, levels, cols), f32),
                pltpu.VMEM((2, levels, cols), f32),
                pltpu.VMEM((2, chunks, rows, CHUNK), bf16),
                pltpu.VMEM((2, 2, chunks, rows, CHUNK), bf16),
                pltpu.VMEM((2, 3 * rows, cols), bf16),
                pltpu.VMEM((2, 3 * rows, cols), bf16),
                pltpu.VMEM((2 * rows, cols + 2 * LANES), bf16),
                pltpu.VMEM((2 * rows, cols + 2 * LANES), bf16),
                pltpu.VMEM((rows, 3 * rows), bf16),
                pltpu.VMEM((2 * rows, 3 * rows), bf16),
                pltpu.VMEM((2 * WIDE, WIDE), bf16),
                pltpu.VMEM((2 * WIDE, WIDE), bf16),
                pltpu.VMEM((chunks, rows, CHUNK), bf16),
                pltpu.SemaphoreType.DMA((3,)),
                pltpu.SemaphoreType.DMA((2,)),
                pltpu.SemaphoreType.DMA((2,)),
                pltpu.SemaphoreType.DMA((2, 2, chunks)),
                pltpu.SemaphoreType.DMA((2, 2, chunks)),
                pltpu.SemaphoreType.DMA((chunks,)),
                pltpu.SemaphoreType.DMA((chunks,)),
            ],
            compiler_params=pltpu.CompilerParams(
                collective_id=0, has_side_effects=True, vmem_limit_bytes=40 * 2**20
            ),
            name="align",
        )(*(pltpu.with_memory_space_constraint(v, pltpu.HBM) for v in (innovation, background, level_weight)))

    placed = (P("member", "row", None), P("member", "row", None), P())
    return jax.shard_map(
        body, mesh=mesh, in_specs=placed, out_specs=P("member", "row", None), check_vma=False
    )
```

```python
import jax
import jax.numpy as jnp
from jax import lax
from jax.experimental import pallas as pl
from jax.experimental.pallas import tpu as pltpu
from jax.sharding import PartitionSpec as P

HALF = 64
SIGMA = 64
LANES = 128
CHUNK = 256
GROUP = 16
WIDE = 256
SCALE = 4096.0


def tap_at(offset):
    grid = lax.broadcasted_iota(jnp.int32, (8, 2 * LANES), 1) - HALF
    off = grid.astype(jnp.float32)
    spread = jnp.float32(SIGMA)
    squares = jnp.where(grid <= HALF, jnp.exp(-off * off / (spread * spread)), 0.0)
    total = jnp.sqrt(jnp.sum(squares[:1], axis=1, keepdims=True))
    value = offset.astype(jnp.float32)
    value = jnp.exp(-value * value / (2.0 * spread * spread)) / total
    return jnp.where(jnp.abs(offset) <= HALF, value, 0.0)


def halves(value):
    high = value.astype(jnp.bfloat16)
    return high, (value - high.astype(jnp.float32)).astype(jnp.bfloat16)


def encode(raw):
    value = raw * SCALE
    value2 = value * value
    value4 = value2 * value2
    value8 = value4 * value4
    return jnp.where(value < 0.0, -value8, value8).astype(jnp.bfloat16)


def decode(code):
    code = code.astype(jnp.float32)
    size = jnp.exp2(jnp.log2(jnp.abs(code)) * 0.125) * (1.0 / SCALE)
    return jnp.where(code < 0.0, -size, size)


def kernel(
    count, inn_hbm, bg_hbm, lw_hbm, out_ref,
    lw_ref, inn, bg, rim, edge_out, edge_in, code_out, code_in, dhigh, dlow,
    mhigh, mlow, whigh, wboth, bhigh, blow,
    in_sem, edge_send, edge_recv, send_sem, recv_sem,
):
    levels, rows, cols = inn.shape
    chunks = cols // CHUNK
    phases = ((1, 2), (0, 3))
    me = lax.axis_index("row")
    has = (me > 0, me < count - 1)
    peer = (jnp.maximum(me - 1, 0), jnp.minimum(me + 1, count - 1))

    load_bg = pltpu.make_async_copy(bg_hbm, bg, in_sem.at[0])
    load_inn = pltpu.make_async_copy(inn_hbm, inn, in_sem.at[1])
    load_bg.start()
    load_inn.start()
    load_lw = pltpu.make_async_copy(lw_hbm, lw_ref, in_sem.at[2])
    load_lw.start()
    barrier = pltpu.get_barrier_semaphore()
    for side in (0, 1):
        @pl.when(has[side])
        def _():
            pl.semaphore_signal(
                barrier, inc=1, device_id={"row": peer[side]},
                device_id_type=pl.DeviceIdType.MESH,
            )

    zeros = jnp.zeros((levels, rows + 16, LANES), jnp.float32)
    rim[:, :, :LANES] = zeros
    rim[:, :, LANES + cols :] = zeros
    strip = jnp.zeros((2 * rows, LANES), jnp.bfloat16)
    for ref in (mhigh, mlow):
        ref[:, :LANES] = strip
        ref[:, LANES + cols :] = strip

    load_bg.wait()
    for level in range(levels):
        edge_out[0, level : level + 1, :] = bg[level, :16, :].astype(jnp.float32)[:1]
        edge_out[1, level : level + 1, :] = bg[level, rows - 16 :, :].astype(jnp.float32)[15:]
    pl.semaphore_wait(barrier, peer[1] - peer[0])

    def edge_copy(side):
        return pltpu.make_async_remote_copy(
            src_ref=edge_out.at[side], dst_ref=edge_in.at[1 - side],
            send_sem=edge_send.at[side], recv_sem=edge_recv.at[1 - side],
            device_id={"row": peer[side]}, device_id_type=pl.DeviceIdType.MESH,
        )

    def code_copy(side, phase, chunk):
        return pltpu.make_async_remote_copy(
            src_ref=code_out.at[phase, chunk], dst_ref=code_in.at[1 - side, phase, chunk],
            send_sem=send_sem.at[side, phase, chunk],
            recv_sem=recv_sem.at[1 - side, phase, chunk],
            device_id={"row": peer[side]}, device_id_type=pl.DeviceIdType.MESH,
        )

    for side in (0, 1):
        @pl.when(has[side])
        def _():
            edge_copy(side).start()

    @pl.loop(0, chunks)
    def _(chunk):
        at = pl.multiple_of(chunk * CHUNK, CHUNK)
        for level in range(levels):
            rim[level, 8 : 8 + rows, pl.ds(LANES + at, CHUNK)] = bg[
                level, :, pl.ds(at, CHUNK)
            ].astype(jnp.float32)

    load_inn.wait()
    load_lw.wait()

    def raw_tile(group, chunk):
        at = chunk * CHUNK
        top = 8 + group * GROUP
        wide = CHUNK + 2 * LANES
        numer_y = numer_x = None
        denom = jnp.ones((GROUP, CHUNK), jnp.float32)
        for level in range(levels):
            weight = lw_ref[level]
            line = rim[level, top : top + GROUP, pl.ds(at, wide)]
            left = pltpu.roll(line, 1, 1)[:, LANES : LANES + CHUNK]
            right = pltpu.roll(line, wide - 1, 1)[:, LANES : LANES + CHUNK]
            above = rim[level, top - 1 : top - 1 + GROUP, pl.ds(LANES + at, CHUNK)]
            below = rim[level, top + 1 : top + 1 + GROUP, pl.ds(LANES + at, CHUNK)]
            grad_x = 0.5 * (right - left)
            grad_y = 0.5 * (below - above)
            span = pl.ds(group * GROUP, GROUP)
            scaled = weight * inn[level, span, pl.ds(at, CHUNK)].astype(jnp.float32)
            part_y, part_x = scaled * grad_y, scaled * grad_x
            numer_y = part_y if numer_y is None else numer_y + part_y
            numer_x = part_x if numer_x is None else numer_x + part_x
            denom = denom + weight * (grad_y * grad_y + grad_x * grad_x)
        inverse = 1.0 / denom
        for comp, numer in enumerate((numer_y, numer_x)):
            raw = numer * inverse
            phase = phases.index([pair for pair in phases if group in pair][0])
            low_row = (2 * comp + phases[phase].index(group)) * GROUP
            code_out[phase, chunk, low_row : low_row + GROUP, :] = encode(raw)
            high, low = halves(raw)
            base = rows + group * GROUP
            dhigh[comp, base : base + GROUP, pl.ds(at, CHUNK)] = high
            dlow[comp, base : base + GROUP, pl.ds(at, CHUNK)] = low

    def send_phase(phase):
        for chunk in range(chunks):
            for group in phases[phase]:
                raw_tile(group, chunk)
            for side in (0, 1):
                @pl.when(has[side])
                def _():
                    code_copy(side, phase, chunk).start()

    send_phase(0)

    for side in (0, 1):
        row = 7 if side == 0 else 8 + rows

        @pl.when(has[side])
        def _():
            edge_copy(1 - side).wait_recv()
            for level in range(levels):
                rim[level, row : row + 1, LANES : LANES + cols] = edge_in[
                    side, level : level + 1, :
                ]

        @pl.when(jnp.logical_not(has[side]))
        def _():
            for level in range(levels):
                rim[level, row : row + 1, LANES : LANES + cols] = jnp.zeros(
                    (1, cols), jnp.float32
                )

    send_phase(1)

    inner = lax.broadcasted_iota(jnp.int32, (2 * WIDE, WIDE), 0)
    outer = lax.broadcasted_iota(jnp.int32, (2 * WIDE, WIDE), 1)
    high, low = halves(tap_at(inner - LANES - outer))
    bhigh[...] = high
    blow[...] = low
    outer = lax.broadcasted_iota(jnp.int32, (rows, 3 * rows), 0)
    inner = lax.broadcasted_iota(jnp.int32, (rows, 3 * rows), 1)
    high, low = halves(tap_at(inner - rows - outer))
    whigh[...] = high
    wboth[:rows] = high
    wboth[rows:] = low
    for side in (0, 1):
        base = 2 * rows * side

        @pl.when(jnp.logical_not(has[side]))
        def _():
            blank = jnp.zeros((2, rows, cols), jnp.bfloat16)
            dhigh[:, base : base + rows, :] = blank
            dlow[:, base : base + rows, :] = blank

    def product(a, b):
        return jnp.dot(a, b, preferred_element_type=jnp.float32)

    def zonal(block):
        at = block * WIDE
        high = mhigh[:, at : at + 2 * WIDE]
        low = mlow[:, at : at + 2 * WIDE]
        total = product(high, bhigh[...]) + product(high, blow[...]) + product(low, bhigh[...])
        out_ref[0, :, at : at + WIDE] = total[:rows]
        out_ref[1, :, at : at + WIDE] = total[rows:]

    def receive(phase, chunk):
        at = chunk * CHUNK
        for side in (0, 1):
            @pl.when(has[side])
            def _():
                code_copy(1 - side, phase, chunk).wait_recv()
                for comp in (0, 1):
                    for order, group in enumerate(phases[phase]):
                        low_row = (2 * comp + order) * GROUP
                        code = code_in[side, phase, chunk, low_row : low_row + GROUP, :]
                        high, low = halves(decode(code))
                        base = 2 * rows * side + group * GROUP
                        dhigh[comp, base : base + GROUP, at : at + CHUNK] = high
                        dlow[comp, base : base + GROUP, at : at + CHUNK] = low

    for chunk in range(chunks):
        receive(0, chunk)
    done = 0
    for chunk in range(chunks):
        at = chunk * CHUNK
        receive(1, chunk)

        for comp in (0, 1):
            both = product(wboth[...], dhigh[comp, :, at : at + CHUNK])
            rest = product(whigh[...], dlow[comp, :, at : at + CHUNK])
            high, low = halves(both[:rows] + (both[rows:] + rest))
            mhigh[comp * rows : (comp + 1) * rows, LANES + at : LANES + at + CHUNK] = high
            mlow[comp * rows : (comp + 1) * rows, LANES + at : LANES + at + CHUNK] = low
        ready = cols // WIDE if chunk == chunks - 1 else ((chunk + 1) * CHUNK - HALF) // WIDE
        for block in range(done, ready):
            zonal(block)
        done = ready

    for side in (0, 1):
        @pl.when(has[side])
        def _():
            edge_copy(side).wait_send()
            for phase in (0, 1):
                for chunk in range(chunks):
                    code_copy(side, phase, chunk).wait_send()


def solution(mesh):
    count = mesh.shape["row"]

    def body(innovation, background, level_weight):
        levels, rows, cols = innovation.shape
        assert rows == HALF and cols % CHUNK == 0
        chunks = cols // CHUNK
        f32, bf16 = jnp.float32, jnp.bfloat16

        def call(*args):
            return kernel(count, *args)

        return pl.pallas_call(
            call,
            out_shape=jax.ShapeDtypeStruct((2, rows, cols), f32),
            in_specs=[
                pl.BlockSpec(memory_space=pltpu.HBM),
                pl.BlockSpec(memory_space=pltpu.HBM),
                pl.BlockSpec(memory_space=pltpu.HBM),
            ],
            out_specs=pl.BlockSpec(memory_space=pltpu.VMEM),
            scratch_shapes=[
                pltpu.SMEM((levels,), f32),
                pltpu.VMEM((levels, rows, cols), bf16),
                pltpu.VMEM((levels, rows, cols), bf16),
                pltpu.VMEM((levels, rows + 16, cols + 2 * LANES), f32),
                pltpu.VMEM((2, levels, cols), f32),
                pltpu.VMEM((2, levels, cols), f32),
                pltpu.VMEM((2, chunks, rows, CHUNK), bf16),
                pltpu.VMEM((2, 2, chunks, rows, CHUNK), bf16),
                pltpu.VMEM((2, 3 * rows, cols), bf16),
                pltpu.VMEM((2, 3 * rows, cols), bf16),
                pltpu.VMEM((2 * rows, cols + 2 * LANES), bf16),
                pltpu.VMEM((2 * rows, cols + 2 * LANES), bf16),
                pltpu.VMEM((rows, 3 * rows), bf16),
                pltpu.VMEM((2 * rows, 3 * rows), bf16),
                pltpu.VMEM((2 * WIDE, WIDE), bf16),
                pltpu.VMEM((2 * WIDE, WIDE), bf16),
                pltpu.SemaphoreType.DMA((3,)),
                pltpu.SemaphoreType.DMA((2,)),
                pltpu.SemaphoreType.DMA((2,)),
                pltpu.SemaphoreType.DMA((2, 2, chunks)),
                pltpu.SemaphoreType.DMA((2, 2, chunks)),
            ],
            compiler_params=pltpu.CompilerParams(
                collective_id=0, has_side_effects=True, vmem_limit_bytes=40 * 2**20
            ),
            name="align",
        )(*(pltpu.with_memory_space_constraint(v, pltpu.HBM) for v in (innovation, background, level_weight)))

    placed = (P("member", "row", None), P("member", "row", None), P())
    return jax.shard_map(
        body, mesh=mesh, in_specs=placed, out_specs=P("member", "row", None), check_vma=False
    )
```

```python
import jax
import jax.numpy as jnp
from jax import lax
from jax.experimental import pallas as pl
from jax.experimental.pallas import tpu as pltpu
from jax.sharding import PartitionSpec as P

HALF = 64
SIGMA = 64
LANES = 128
CHUNK = 1024
GROUP = 16
WIDE = 256
SCALE = 4096.0


def tap_at(offset):
    grid = lax.broadcasted_iota(jnp.int32, (8, 2 * LANES), 1) - HALF
    off = grid.astype(jnp.float32)
    spread = jnp.float32(SIGMA)
    squares = jnp.where(grid <= HALF, jnp.exp(-off * off / (spread * spread)), 0.0)
    total = jnp.sqrt(jnp.sum(squares[:1], axis=1, keepdims=True))
    value = offset.astype(jnp.float32)
    value = jnp.exp(-value * value / (2.0 * spread * spread)) / total
    return jnp.where(jnp.abs(offset) <= HALF, value, 0.0)


def halves(value):
    high = value.astype(jnp.bfloat16)
    return high, (value - high.astype(jnp.float32)).astype(jnp.bfloat16)


def encode(raw):
    value = raw * SCALE
    value2 = value * value
    value4 = value2 * value2
    value8 = value4 * value4
    return jnp.where(value < 0.0, -value8, value8).astype(jnp.bfloat16)


def decode(code):
    code = code.astype(jnp.float32)
    size = jnp.exp2(jnp.log2(jnp.abs(code)) * 0.125) * (1.0 / SCALE)
    return jnp.where(code < 0.0, -size, size)


def kernel(
    count, inn_hbm, bg_hbm, lw_hbm, out_ref,
    lw_ref, inn, bg, rim, edge_out, edge_in, code_out, code_in, dhigh, dlow,
    mhigh, mlow, whigh, wboth, bhigh, blow,
    in_sem, edge_send, edge_recv, send_sem, recv_sem,
):
    levels, rows, cols = inn.shape
    chunks = cols // CHUNK
    phases = ((1, 2), (0, 3))
    me = lax.axis_index("row")
    has = (me > 0, me < count - 1)
    peer = (jnp.maximum(me - 1, 0), jnp.minimum(me + 1, count - 1))

    load_bg = pltpu.make_async_copy(bg_hbm, bg, in_sem.at[0])
    load_inn = pltpu.make_async_copy(inn_hbm, inn, in_sem.at[1])
    load_bg.start()
    load_inn.start()
    load_lw = pltpu.make_async_copy(lw_hbm, lw_ref, in_sem.at[2])
    load_lw.start()
    barrier = pltpu.get_barrier_semaphore()
    for side in (0, 1):
        @pl.when(has[side])
        def _():
            pl.semaphore_signal(
                barrier, inc=1, device_id={"row": peer[side]},
                device_id_type=pl.DeviceIdType.MESH,
            )

    zeros = jnp.zeros((levels, rows + 16, LANES), jnp.float32)
    rim[:, :, :LANES] = zeros
    rim[:, :, LANES + cols :] = zeros
    strip = jnp.zeros((2 * rows, LANES), jnp.bfloat16)
    for ref in (mhigh, mlow):
        ref[:, :LANES] = strip
        ref[:, LANES + cols :] = strip

    load_bg.wait()
    for level in range(levels):
        edge_out[0, level : level + 1, :] = bg[level, :16, :].astype(jnp.float32)[:1]
        edge_out[1, level : level + 1, :] = bg[level, rows - 16 :, :].astype(jnp.float32)[15:]
    pl.semaphore_wait(barrier, peer[1] - peer[0])

    def edge_copy(side):
        return pltpu.make_async_remote_copy(
            src_ref=edge_out.at[side], dst_ref=edge_in.at[1 - side],
            send_sem=edge_send.at[side], recv_sem=edge_recv.at[1 - side],
            device_id={"row": peer[side]}, device_id_type=pl.DeviceIdType.MESH,
        )

    def code_copy(side, phase, chunk):
        return pltpu.make_async_remote_copy(
            src_ref=code_out.at[phase, chunk], dst_ref=code_in.at[1 - side, phase, chunk],
            send_sem=send_sem.at[side, phase, chunk],
            recv_sem=recv_sem.at[1 - side, phase, chunk],
            device_id={"row": peer[side]}, device_id_type=pl.DeviceIdType.MESH,
        )

    for side in (0, 1):
        @pl.when(has[side])
        def _():
            edge_copy(side).start()

    @pl.loop(0, chunks)
    def _(chunk):
        at = pl.multiple_of(chunk * CHUNK, CHUNK)
        for level in range(levels):
            rim[level, 8 : 8 + rows, pl.ds(LANES + at, CHUNK)] = bg[
                level, :, pl.ds(at, CHUNK)
            ].astype(jnp.float32)

    load_inn.wait()
    load_lw.wait()

    def raw_tile(group, chunk):
        at = chunk * CHUNK
        top = 8 + group * GROUP
        wide = CHUNK + 2 * LANES
        numer_y = numer_x = None
        denom = jnp.ones((GROUP, CHUNK), jnp.float32)
        for level in range(levels):
            weight = lw_ref[level]
            line = rim[level, top : top + GROUP, pl.ds(at, wide)]
            left = pltpu.roll(line, 1, 1)[:, LANES : LANES + CHUNK]
            right = pltpu.roll(line, wide - 1, 1)[:, LANES : LANES + CHUNK]
            above = rim[level, top - 1 : top - 1 + GROUP, pl.ds(LANES + at, CHUNK)]
            below = rim[level, top + 1 : top + 1 + GROUP, pl.ds(LANES + at, CHUNK)]
            grad_x = 0.5 * (right - left)
            grad_y = 0.5 * (below - above)
            span = pl.ds(group * GROUP, GROUP)
            scaled = weight * inn[level, span, pl.ds(at, CHUNK)].astype(jnp.float32)
            part_y, part_x = scaled * grad_y, scaled * grad_x
            numer_y = part_y if numer_y is None else numer_y + part_y
            numer_x = part_x if numer_x is None else numer_x + part_x
            denom = denom + weight * (grad_y * grad_y + grad_x * grad_x)
        inverse = 1.0 / denom
        for comp, numer in enumerate((numer_y, numer_x)):
            raw = numer * inverse
            phase = phases.index([pair for pair in phases if group in pair][0])
            low_row = (2 * comp + phases[phase].index(group)) * GROUP
            code_out[phase, chunk, low_row : low_row + GROUP, :] = encode(raw)
            high, low = halves(raw)
            base = rows + group * GROUP
            dhigh[comp, base : base + GROUP, pl.ds(at, CHUNK)] = high
            dlow[comp, base : base + GROUP, pl.ds(at, CHUNK)] = low

    def send_phase(phase):
        for chunk in range(chunks):
            for group in phases[phase]:
                raw_tile(group, chunk)
            for side in (0, 1):
                @pl.when(has[side])
                def _():
                    code_copy(side, phase, chunk).start()

    send_phase(0)

    for side in (0, 1):
        row = 7 if side == 0 else 8 + rows

        @pl.when(has[side])
        def _():
            edge_copy(1 - side).wait_recv()
            for level in range(levels):
                rim[level, row : row + 1, LANES : LANES + cols] = edge_in[
                    side, level : level + 1, :
                ]

        @pl.when(jnp.logical_not(has[side]))
        def _():
            for level in range(levels):
                rim[level, row : row + 1, LANES : LANES + cols] = jnp.zeros(
                    (1, cols), jnp.float32
                )

    send_phase(1)

    inner = lax.broadcasted_iota(jnp.int32, (2 * WIDE, WIDE), 0)
    outer = lax.broadcasted_iota(jnp.int32, (2 * WIDE, WIDE), 1)
    high, low = halves(tap_at(inner - LANES - outer))
    bhigh[...] = high
    blow[...] = low
    outer = lax.broadcasted_iota(jnp.int32, (rows, 3 * rows), 0)
    inner = lax.broadcasted_iota(jnp.int32, (rows, 3 * rows), 1)
    high, low = halves(tap_at(inner - rows - outer))
    whigh[...] = high
    wboth[:rows] = high
    wboth[rows:] = low
    for side in (0, 1):
        base = 2 * rows * side

        @pl.when(jnp.logical_not(has[side]))
        def _():
            blank = jnp.zeros((2, rows, cols), jnp.bfloat16)
            dhigh[:, base : base + rows, :] = blank
            dlow[:, base : base + rows, :] = blank

    def product(a, b):
        return jnp.dot(a, b, preferred_element_type=jnp.float32)

    def zonal(block):
        at = block * WIDE
        high = mhigh[:, at : at + 2 * WIDE]
        low = mlow[:, at : at + 2 * WIDE]
        total = product(high, bhigh[...]) + product(high, blow[...]) + product(low, bhigh[...])
        out_ref[0, :, at : at + WIDE] = total[:rows]
        out_ref[1, :, at : at + WIDE] = total[rows:]

    def receive(phase, chunk):
        at = chunk * CHUNK
        for side in (0, 1):
            @pl.when(has[side])
            def _():
                code_copy(1 - side, phase, chunk).wait_recv()
                for comp in (0, 1):
                    for order, group in enumerate(phases[phase]):
                        low_row = (2 * comp + order) * GROUP
                        code = code_in[side, phase, chunk, low_row : low_row + GROUP, :]
                        high, low = halves(decode(code))
                        base = 2 * rows * side + group * GROUP
                        dhigh[comp, base : base + GROUP, at : at + CHUNK] = high
                        dlow[comp, base : base + GROUP, at : at + CHUNK] = low

    for chunk in range(chunks):
        receive(0, chunk)
    done = 0
    for chunk in range(chunks):
        at = chunk * CHUNK
        receive(1, chunk)

        for comp in (0, 1):
            both = product(wboth[...], dhigh[comp, :, at : at + CHUNK])
            rest = product(whigh[...], dlow[comp, :, at : at + CHUNK])
            high, low = halves(both[:rows] + (both[rows:] + rest))
            mhigh[comp * rows : (comp + 1) * rows, LANES + at : LANES + at + CHUNK] = high
            mlow[comp * rows : (comp + 1) * rows, LANES + at : LANES + at + CHUNK] = low
        ready = cols // WIDE if chunk == chunks - 1 else ((chunk + 1) * CHUNK - HALF) // WIDE
        for block in range(done, ready):
            zonal(block)
        done = ready

    for side in (0, 1):
        @pl.when(has[side])
        def _():
            edge_copy(side).wait_send()
            for phase in (0, 1):
                for chunk in range(chunks):
                    code_copy(side, phase, chunk).wait_send()


def solution(mesh):
    count = mesh.shape["row"]

    def body(innovation, background, level_weight):
        levels, rows, cols = innovation.shape
        assert rows == HALF and cols % CHUNK == 0
        chunks = cols // CHUNK
        f32, bf16 = jnp.float32, jnp.bfloat16

        def call(*args):
            return kernel(count, *args)

        return pl.pallas_call(
            call,
            out_shape=jax.ShapeDtypeStruct((2, rows, cols), f32),
            in_specs=[
                pl.BlockSpec(memory_space=pltpu.HBM),
                pl.BlockSpec(memory_space=pltpu.HBM),
                pl.BlockSpec(memory_space=pltpu.HBM),
            ],
            out_specs=pl.BlockSpec(memory_space=pltpu.VMEM),
            scratch_shapes=[
                pltpu.SMEM((levels,), f32),
                pltpu.VMEM((levels, rows, cols), bf16),
                pltpu.VMEM((levels, rows, cols), bf16),
                pltpu.VMEM((levels, rows + 16, cols + 2 * LANES), f32),
                pltpu.VMEM((2, levels, cols), f32),
                pltpu.VMEM((2, levels, cols), f32),
                pltpu.VMEM((2, chunks, rows, CHUNK), bf16),
                pltpu.VMEM((2, 2, chunks, rows, CHUNK), bf16),
                pltpu.VMEM((2, 3 * rows, cols), bf16),
                pltpu.VMEM((2, 3 * rows, cols), bf16),
                pltpu.VMEM((2 * rows, cols + 2 * LANES), bf16),
                pltpu.VMEM((2 * rows, cols + 2 * LANES), bf16),
                pltpu.VMEM((rows, 3 * rows), bf16),
                pltpu.VMEM((2 * rows, 3 * rows), bf16),
                pltpu.VMEM((2 * WIDE, WIDE), bf16),
                pltpu.VMEM((2 * WIDE, WIDE), bf16),
                pltpu.SemaphoreType.DMA((3,)),
                pltpu.SemaphoreType.DMA((2,)),
                pltpu.SemaphoreType.DMA((2,)),
                pltpu.SemaphoreType.DMA((2, 2, chunks)),
                pltpu.SemaphoreType.DMA((2, 2, chunks)),
            ],
            compiler_params=pltpu.CompilerParams(
                collective_id=0, has_side_effects=True, vmem_limit_bytes=40 * 2**20
            ),
            name="align",
        )(*(pltpu.with_memory_space_constraint(v, pltpu.HBM) for v in (innovation, background, level_weight)))

    placed = (P("member", "row", None), P("member", "row", None), P())
    return jax.shard_map(
        body, mesh=mesh, in_specs=placed, out_specs=P("member", "row", None), check_vma=False
    )
```
